512 devices in a mesh: pipe: 16 (over y, core), expert: 32 (over x, z).
Axes of the slice: x: 4, y: 8, z: 8, core: 2. Of those that a mesh axis runs over, the one named last changes fastest.
Arguments:
- fwd_state: bfloat16 [16, 2048, 2048], P('pipe', 'expert'), may hold values from -6 to 6
- rev_state: bfloat16 [16, 2048, 2048], P('pipe', 'expert'), may hold values from -6 to 6
- norm_gain: float32 [16, 2048], P('pipe'), may hold values from 0.1 to 1.9
- gate_weight: bfloat16 [16, 2048, 6144], P('pipe', None, 'expert'), may hold values from -0.125 to 0.125
- up_weight: bfloat16 [16, 2048, 6144], P('pipe', None, 'expert'), may hold values from -0.125 to 0.125
- down_weight: bfloat16 [16, 6144, 2048], P('pipe', 'expert'), may hold values from -0.21875 to 0.21875
- fwd_routes: int32 [2, 16, 2048, 2], P(None, 'pipe', 'expert'), may hold values from 0 to 7, all different within a row; in each aligned block of 64 rows (0 to 63, 64 to 127, ..., all dimensions but the last counted through in order) at most 24 rows name the same one
- rev_routes: int32 [2, 16, 2048, 2], P(None, 'pipe', 'expert'), may hold values from 0 to 7, all different within a row; in each aligned block of 64 rows (0 to 63, 64 to 127, ..., all dimensions but the last counted through in order) at most 24 rows name the same one
- fwd_combine: float32 [2, 16, 2048, 2], P(None, 'pipe', 'expert'), may hold values from 0.2 to 1
- rev_combine: float32 [2, 16, 2048, 2], P(None, 'pipe', 'expert'), may hold values from 0.2 to 1
Outputs:
- fwd_out: bfloat16 [16, 2048, 2048], P('pipe', 'expert')
- rev_out: bfloat16 [16, 2048, 2048], P('pipe', 'expert')
The draws below stay inside these ranges and needn't reach their ends.
Inputs may be any that keep to these rules, and one draw needn't show every extreme that they name: `fwd_routes`: each token's 2 ids are distinct. In each aligned block of 64 tokens (one device's tokens for one application and section) no expert is chosen by more than 24 tokens, a bound that some block reaches; every expert is chosen somewhere. `rev_routes`: as for fwd_routes.
All inputs are finite; a program needn't handle non-finite values.
Results may differ from the reference program's by a relative error of at most 0.0068.
Values may be sent and summed in bfloat16 or wider, within the bound.
A program may use at most 128 MiB of HBM per device.

```python
import math
import jax
import jax.numpy as jnp
import numpy as np
from jax import lax

D = 2048
FF = 768
EXPERTS = 8
TOPK = 2
TICKS = 2
TOK_DEV = 64
GROUP = 4
CAP = 24
TOKENS = 2048
N_PIPE = 16
N_EXPERT = 32


def block_levels(stream_key, shape, shards, smallest, largest):
    level = 1.0
    for dim, shards_of in shards:
        steps = jax.random.uniform(jax.random.fold_in(jax.random.fold_in(stream_key, 6), dim), (shards_of,), jnp.float32, smallest / len(shards), largest / len(shards))
        level = level * jnp.repeat(jnp.exp(steps), shape[dim] // shards_of).reshape((-1,) + (1,) * (len(shape) - 1 - dim))
    return level


def routed_block(rng, own, number, rows, count, top, reach, skew):
    order = jax.random.permutation(rng, count)
    heavy_load, usual = portions_of(count, rows * top, reach, skew, True), portions_of(count, rows * top, reach, skew, False)
    places = jnp.arange(count)

    def named(sizes, turn):
        used = int((sizes > 0).sum())
        fixed = max(1, used // 4)
        shifted = fixed + (places - fixed + turn * (used - fixed)) % max(1, count - fixed)
        return jnp.zeros((count,), jnp.int32).at[order[jnp.where(places < fixed, places, shifted)]].set(jnp.asarray(sizes, jnp.int32))

    sizes = jnp.where(number % 4 == 0, named(heavy_load, number // 4), named(usual, number - number // 4 - 1))
    mixed = jax.random.permutation(jax.random.fold_in(own, 3), count)
    giver, receiver = mixed[0:count // 2 * 2:2], mixed[1:count // 2 * 2:2]
    margin = jnp.minimum(sizes[giver] - 1, reach - sizes[receiver]) // 2
    margin = jnp.where((giver == order[0]) | (receiver == order[0]) | (sizes[receiver] == 0), 0, jnp.maximum(margin, 0))
    shifted = jax.random.randint(jax.random.fold_in(own, 4), (count // 2,), 0, 1 << 20) % (margin + 1)
    sizes = sizes.at[giver].add(-shifted).at[receiver].add(shifted)
    members = jnp.searchsorted(jnp.cumsum(sizes), jnp.arange(rows * top), side="right").astype(jnp.int32)
    listing = members.reshape(top, rows).T
    listing = listing[jax.random.permutation(jax.random.fold_in(own, 1), rows)]
    turn = jax.random.randint(jax.random.fold_in(own, 2), (rows, 1), 0, top)
    return jnp.take_along_axis(listing, (jnp.arange(top)[None, :] + turn) % top, axis=1)


def portions_of(amount, total, most, lean, full):
    portions = [(1 << 20) // math.isqrt(grade ** lean) + 1 for grade in range(1, amount + 1)]
    largest = most if full else min(most, max(-(-total // amount), total * portions[0] // sum(portions)))
    least = 1 if total - largest >= amount - 1 else 0
    holding, spare = [largest] + [least] * (amount - 1), total - largest - least * (amount - 1)
    while spare > 0:
        free = [i for i in range(1, amount) if holding[i] < largest] or [i for i in range(1, amount) if holding[i] < most]
        whole, budget = sum([portions[i] for i in free]), spare
        for i in free:
            extra = min(most - holding[i], max(1, budget * portions[i] // whole), spare)
            holding[i] = holding[i] + extra
            spare = spare - extra
    return np.array(holding)


def gaussian(stream_key, dims, deviation, limit, cuts=(), held_as=jnp.bfloat16):
    loudness = block_levels(stream_key, dims, cuts, -0.22, 0.18) if cuts else 1.0
    array = jax.random.normal(stream_key, dims, jnp.float32) * deviation * loudness
    return jnp.minimum(jnp.maximum(array, -limit), limit).astype(held_as)


def setup_inputs(seed: int = 0) -> dict:
    splits = jax.random.split(jax.random.key(seed), 11)
    fwd_state = gaussian(splits[0], (N_PIPE, TOKENS, D), 1.0, 6.0, ((0, 16), (1, 32)))
    rev_state = gaussian(splits[1], (N_PIPE, TOKENS, D), 1.0, 6.0, ((0, 16), (1, 32)))
    norm_gain = jnp.clip(1.0 + 0.18 * jax.random.normal(splits[2], (N_PIPE, D), jnp.float32), 0.1, 1.9)
    gate_weight = gaussian(splits[3], (N_PIPE, D, EXPERTS * FF), D ** -0.5, 0.125, ((0, 16), (2, 32)))
    up_weight = gaussian(splits[4], (N_PIPE, D, EXPERTS * FF), D ** -0.5, 0.125, ((0, 16), (2, 32)))
    down_weight = gaussian(splits[5], (N_PIPE, EXPERTS * FF, D), FF ** -0.5, 0.21875, ((0, 16), (1, 32)))
    fwd_routes_keys = jax.random.split(jax.random.fold_in(splits[6], 1), TICKS * N_PIPE * TOKENS // TOK_DEV)
    fwd_routes_turns = jax.random.permutation(jax.random.fold_in(splits[6], 3), TICKS * N_PIPE * TOKENS // TOK_DEV)
    fwd_routes = jax.vmap(lambda own, number: routed_block(jax.random.fold_in(splits[6], 2), own, number, TOK_DEV, EXPERTS, TOPK, CAP, 2))(fwd_routes_keys, fwd_routes_turns).reshape((TICKS, N_PIPE, TOKENS, TOPK))
    rev_routes_keys = jax.random.split(jax.random.fold_in(splits[7], 1), TICKS * N_PIPE * TOKENS // TOK_DEV)
    rev_routes_turns = jax.random.permutation(jax.random.fold_in(splits[7], 3), TICKS * N_PIPE * TOKENS // TOK_DEV)
    rev_routes = jax.vmap(lambda own, number: routed_block(jax.random.fold_in(splits[7], 2), own, number, TOK_DEV, EXPERTS, TOPK, CAP, 2))(rev_routes_keys, rev_routes_turns).reshape((TICKS, N_PIPE, TOKENS, TOPK))
    fwd_combine = jnp.clip(jnp.exp(math.log(1.0) - 1.609438 * jax.random.uniform(splits[8], (TICKS, N_PIPE, TOKENS, TOPK), jnp.float32) ** block_levels(splits[8], (TICKS, N_PIPE, TOKENS, TOPK), ((1, 16), (2, 32)), -0.2, 0.2)), 0.2, 1.0)
    rev_combine = jnp.clip(jnp.exp(math.log(1.0) - 1.609438 * jax.random.uniform(splits[9], (TICKS, N_PIPE, TOKENS, TOPK), jnp.float32) ** block_levels(splits[9], (TICKS, N_PIPE, TOKENS, TOPK), ((1, 16), (2, 32)), -0.2, 0.2)), 0.2, 1.0)
    return {"fwd_state": fwd_state, "rev_state": rev_state, "norm_gain": norm_gain, "gate_weight": gate_weight, "up_weight": up_weight, "down_weight": down_weight, "fwd_routes": fwd_routes, "rev_routes": rev_routes, "fwd_combine": fwd_combine, "rev_combine": rev_combine}


def expert_pass(items):
    rows_in, gate_cols, up_cols, down_rows = items
    gate_act = jnp.dot(rows_in, gate_cols, preferred_element_type=jnp.float32)
    up_act = jnp.dot(rows_in, up_cols, preferred_element_type=jnp.float32)
    activated = (jax.nn.silu(gate_act) * up_act).astype(jnp.bfloat16)
    piece_width = FF // GROUP
    pieces = jnp.einsum('rgh,ghd->grd', activated.reshape(-1, GROUP, piece_width).astype(jnp.float32), down_rows.reshape(GROUP, piece_width, D).astype(jnp.float32))
    rounded = lax.optimization_barrier(pieces.astype(jnp.bfloat16))
    return lax.optimization_barrier(jnp.sum(rounded.astype(jnp.float32), axis=0))

def section_layer(items):
    hidden, gain_row, gate_all, up_all, down_all, route_ids, route_weights = items
    widened = hidden.astype(jnp.float32)
    scale_inv = lax.rsqrt(lax.optimization_barrier(jnp.mean(widened * widened, axis=-1, keepdims=True)) + 1e-06)
    normed = (widened * scale_inv * gain_row).astype(jnp.bfloat16)
    flat_ids = route_ids.reshape(N_EXPERT, TOK_DEV * TOPK).astype(jnp.int32)
    expert_hot = (flat_ids[:, :, None] == jnp.arange(EXPERTS, dtype=jnp.int32)[None, None, :]).astype(jnp.int32)
    before = jnp.cumsum(expert_hot, axis=1) - expert_hot
    slot_rank = lax.optimization_barrier(jnp.sum(before * expert_hot, axis=2))
    source = jnp.arange(N_EXPERT, dtype=jnp.int32)[:, None]
    position = (flat_ids * (N_EXPERT * CAP) + source * CAP + slot_rank).reshape(-1).astype(jnp.int32)
    repeated = jnp.repeat(normed, TOPK, axis=0)
    buffers = jnp.zeros((EXPERTS * N_EXPERT * CAP, D), jnp.bfloat16).at[position].set(repeated)
    gate_split = gate_all.reshape(D, EXPERTS, FF).transpose(1, 0, 2)
    up_split = up_all.reshape(D, EXPERTS, FF).transpose(1, 0, 2)
    down_split = down_all.reshape(EXPERTS, FF, D)
    results = lax.map(expert_pass, (buffers.reshape(EXPERTS, N_EXPERT * CAP, D), gate_split, up_split, down_split))
    route_out = results.reshape(-1, D)[position]
    expert_out = lax.optimization_barrier(jnp.sum(route_out.reshape(TOKENS, TOPK, D) * route_weights[:, :, None], axis=1))
    return (widened + expert_out).astype(jnp.bfloat16)

def reference(fwd_state, rev_state, norm_gain, gate_weight, up_weight, down_weight, fwd_routes, rev_routes, fwd_combine, rev_combine):
    for tick_index in range(TICKS):
        fwd_out = lax.map(section_layer, (fwd_state, norm_gain, gate_weight, up_weight, down_weight, fwd_routes[tick_index], fwd_combine[tick_index]))
        rev_out = lax.map(section_layer, (rev_state, norm_gain, gate_weight, up_weight, down_weight, rev_routes[tick_index], rev_combine[tick_index]))
        if tick_index + 1 < TICKS:
            fwd_state = jnp.roll(fwd_out, 1, axis=0)
            rev_state = jnp.roll(rev_out, -1, axis=0)
    return (fwd_out, rev_out)
```

```python
import jax
import jax.numpy as jnp
from jax import lax
from jax.sharding import PartitionSpec as P

EXPERTS = 8
TICKS = 2
CAP = 24
NX = 4
NZ = 8


def from_behind(block, axis, distance):
    devices = range(lax.axis_size(axis))
    route = [((i - distance) % len(devices), i) for i in devices]
    return lax.ppermute(block, axis, route)


def along_x(block, distance):
    route = [
        (x * NZ + z, ((x + distance) % NX) * NZ + z) for x in range(NX) for z in range(NZ)
    ]
    return lax.ppermute(block, "expert", route)


Z_GROUPS = [[x * NZ + z for z in range(NZ)] for x in range(NX)]


def normed_rows(hidden, gain_row):
    widened = hidden.astype(jnp.float32)
    scale_inv = lax.rsqrt(jnp.mean(widened * widened, axis=-1, keepdims=True) + 1e-06)
    return (widened * scale_inv * gain_row).astype(jnp.bfloat16)


def routing(ids, weights, x_index, half):
    tok = ids.shape[-1]
    wanted = 2 * ((x_index + jnp.arange(NX, dtype=jnp.int32)) % NX) + half
    match = ids[None] == wanted[:, None, None, None]
    weight = jnp.sum(jnp.where(match, weights[None], 0.0), axis=2)
    chosen = jnp.any(match, axis=2)
    count = chosen.astype(jnp.int32)
    rank = jnp.cumsum(count, axis=-1) - count
    slot = jnp.arange(CAP, dtype=jnp.int32)
    hot = chosen[:, :, None, :] & (rank[:, :, None, :] == slot[None, None, :, None])
    same = jnp.eye(NZ, dtype=jnp.bool_)
    block = hot[:, :, :, None, :] & same[None, :, None, :, None]
    pick = block.astype(jnp.bfloat16).reshape(NX * NZ * CAP, NZ * tok)
    high = lax.reduce_precision(weight, 8, 7)
    low = weight - high
    parts = []
    for part in (high, low):
        spread = jnp.where(block, part[:, :, None, None, :], 0.0).astype(jnp.bfloat16)
        parts.append(spread.reshape(NX * NZ * CAP, NZ * tok))
    return pick, parts


def exchange(blocks):
    middle = blocks[2].shape[0] // 2
    one = along_x(blocks[1], 1)
    three = along_x(blocks[3], -1)
    first = along_x(blocks[2][:middle], 1)
    second = along_x(blocks[2][middle:], -1)
    first = along_x(first, 1)
    second = along_x(second, -1)
    return [blocks[0], one, jnp.concatenate([first, second]), three]


def expert_rows(rows, gate_local, up_local, down_local):
    gate_act = jnp.dot(rows, gate_local, preferred_element_type=jnp.float32)
    up_act = jnp.dot(rows, up_local, preferred_element_type=jnp.float32)
    activated = (jax.nn.silu(gate_act) * up_act).astype(jnp.bfloat16)
    return jnp.dot(activated, down_local, preferred_element_type=jnp.float32).astype(jnp.bfloat16)


def gather_z(rows):
    return lax.all_gather(rows, "expert", axis_index_groups=Z_GROUPS, axis=0, tiled=True)


def scatter_z(rows):
    return lax.psum_scatter(
        rows, "expert", scatter_dimension=0, axis_index_groups=Z_GROUPS, tiled=True
    )


def section_layer(hidden, plan, gain_row, gate_local, up_local, down_local):
    pick, parts = plan
    normed = gather_z(normed_rows(hidden, gain_row))
    width = normed.shape[1]
    picked = jnp.dot(pick, normed, preferred_element_type=jnp.float32).astype(jnp.bfloat16)
    rows = jnp.concatenate(exchange(list(picked.reshape(NX, -1, width))))
    out = expert_rows(rows, gate_local, up_local, down_local).reshape(NX, -1, width)
    back = exchange([out[0], out[3], out[2], out[1]])
    back = jnp.concatenate([back[0], back[3], back[2], back[1]])
    dims = (((0,), (0,)), ((), ()))
    moe = sum(
        lax.dot_general(part, back, dims, preferred_element_type=jnp.float32) for part in parts
    )
    moe = scatter_z(moe.astype(jnp.bfloat16))
    return (hidden.astype(jnp.float32) + moe.astype(jnp.float32)).astype(jnp.bfloat16)


def body(
    fwd_state,
    rev_state,
    norm_gain,
    gate_weight,
    up_weight,
    down_weight,
    fwd_routes,
    rev_routes,
    fwd_combine,
    rev_combine,
):
    index = lax.axis_index("expert")
    x_index = index // NZ
    half = (index % NZ) // (NZ // 2)
    gain_row = norm_gain[0]
    weights = (gate_weight[0], up_weight[0], down_weight[0])
    tok = fwd_state.shape[1]
    tables = [a[:, 0].astype(jnp.float32) for a in (fwd_routes, rev_routes, fwd_combine, rev_combine)]
    table = jnp.stack(tables).transpose(0, 1, 3, 2).reshape(-1, tok)
    table = gather_z(table).reshape(NZ, 4, TICKS, 2, tok)
    now = [fwd_state[0], rev_state[0]]
    for tick in range(TICKS):
        nxt = []
        for stream in range(2):
            plan = routing(
                table[:, stream, tick].astype(jnp.int32),
                table[:, 2 + stream, tick],
                x_index,
                half,
            )
            nxt.append(section_layer(now[stream], plan, gain_row, *weights))
        if tick + 1 < TICKS:
            now = [from_behind(nxt[0], "pipe", 1), from_behind(nxt[1], "pipe", -1)]
    return (nxt[0][None], nxt[1][None])


def solution(mesh):
    placed = (
        P("pipe", "expert", None),
        P("pipe", "expert", None),
        P("pipe", None),
        P("pipe", None, "expert"),
        P("pipe", None, "expert"),
        P("pipe", "expert", None),
        P(None, "pipe", "expert", None),
        P(None, "pipe", "expert", None),
        P(None, "pipe", "expert", None),
        P(None, "pipe", "expert", None),
    )
    return jax.shard_map(
        body,
        mesh=mesh,
        in_specs=placed,
        out_specs=(P("pipe", "expert", None), P("pipe", "expert", None)),
        check_vma=False,
    )
```

```python
import functools

import jax
import jax.numpy as jnp
from jax import lax
from jax.experimental import pallas as pl
from jax.experimental.pallas import tpu as pltpu
from jax.sharding import PartitionSpec as P

TICKS = 2
CAP = 24
NX = 4
NZ = 8
RING = 4


def from_behind(block, axis, distance):
    devices = range(lax.axis_size(axis))
    route = [((i - distance) % len(devices), i) for i in devices]
    return lax.ppermute(block, axis, route)


def from_partner(block):
    return lax.ppermute(block, "expert", [(i, i ^ 1) for i in range(NX * NZ)])


def neighbours(axis):
    me = lax.axis_index("expert")
    x, z = me // NZ, me % NZ
    if axis == "x":
        return ((x + 1) % NX) * NZ + z, ((x + NX - 1) % NX) * NZ + z
    return x * NZ + (z + 2) % NZ, x * NZ + (z + NZ - 2) % NZ


def exchange_kernel(jobs, *refs):
    count = len(jobs)
    ins, outs = refs[:count], refs[count : 2 * count]
    relays = refs[2 * count : 3 * count]
    send, recv = refs[3 * count :]
    rings = {axis: neighbours(axis) for axis in dict.fromkeys(axis for axis, _ in jobs)}
    barrier = pltpu.get_barrier_semaphore()
    for pair in rings.values():
        for other in pair:
            pl.semaphore_signal(
                barrier,
                inc=1,
                device_id={"expert": other},
                device_id_type=pl.DeviceIdType.MESH,
            )
    pl.semaphore_wait(barrier, 2 * len(rings))

    def copy(job, number, src, dst, way):
        return pltpu.make_async_remote_copy(
            src_ref=src,
            dst_ref=dst,
            send_sem=send.at[job, number],
            recv_sem=recv.at[job, number],
            device_id={"expert": rings[jobs[job][0]][way]},
            device_id_type=pl.DeviceIdType.MESH,
        )

    first, later, direct = [], [], []
    for job, (_, kind) in enumerate(jobs):
        src, dst, relay = ins[job], outs[job], relays[job]
        rows = dst.shape[1]
        low, high = pl.ds(0, rows // 2), pl.ds(rows // 2, rows // 2)
        if kind == "gather":
            first.append(copy(job, 0, src.at[low], dst.at[1, low], 0))
            first.append(copy(job, 1, src.at[high], dst.at[3, high], 1))
            direct.append(copy(job, 2, src.at[high], dst.at[1, high], 0))
            direct.append(copy(job, 3, src.at[low], dst.at[3, low], 1))
            later.append(copy(job, 4, dst.at[1, low], dst.at[2, low], 0))
            later.append(copy(job, 5, dst.at[3, high], dst.at[2, high], 1))
        else:
            there, back = (0, 1) if kind == "swap" else (1, 0)
            first.append(copy(job, 0, src.at[2, low], relay.at[0], 0))
            first.append(copy(job, 1, src.at[2, high], relay.at[1], 1))
            direct.append(copy(job, 2, src.at[1], dst.at[1], there))
            direct.append(copy(job, 3, src.at[3], dst.at[3], back))
            later.append(copy(job, 4, relay.at[0], dst.at[2, low], 0))
            later.append(copy(job, 5, relay.at[1], dst.at[2, high], 1))
    for one in first + direct:
        one.start()
    for job, (_, kind) in enumerate(jobs):
        outs[job][0] = ins[job][...] if kind == "gather" else ins[job][0]
    for early, late in zip(first, later):
        early.wait_recv()
        late.start()
    for one in first:
        one.wait_send()
    for one in direct + later:
        one.wait()


def exchange(number, jobs, *arrays):
    shapes, relays, sent = [], [], 0
    for (_, kind), array in zip(jobs, arrays):
        rows, width = array.shape[-2:]
        shapes.append(jax.ShapeDtypeStruct((RING, rows, width), array.dtype))
        relays.append(pltpu.VMEM((2, rows // 2, width), array.dtype))
        sent += 4 * rows * width * 2
    whole = pl.BlockSpec(memory_space=pltpu.VMEM)
    return pl.pallas_call(
        functools.partial(exchange_kernel, jobs),
        out_shape=shapes,
        in_specs=[whole] * len(jobs),
        out_specs=[whole] * len(jobs),
        scratch_shapes=relays
        + [pltpu.SemaphoreType.DMA((len(jobs), 6)), pltpu.SemaphoreType.DMA((len(jobs), 6))],
        cost_estimate=pl.CostEstimate(flops=0, bytes_accessed=64_000_000, transcendentals=0),
        compiler_params=pltpu.CompilerParams(collective_id=number, has_side_effects=True),
    )(*arrays)


def normed_rows(hidden, gain_row):
    widened = hidden.astype(jnp.float32)
    scale_inv = lax.rsqrt(jnp.mean(widened * widened, axis=-1, keepdims=True) + 1e-06)
    return (widened * scale_inv * gain_row).astype(jnp.bfloat16)


def routing(ids, weights, x_index, half):
    tok = ids.shape[-1]
    wanted = 2 * ((x_index + jnp.arange(NX, dtype=jnp.int32)) % NX) + half
    match = ids[None] == wanted[:, None, None, None]
    weight = jnp.sum(jnp.where(match, weights[None], 0.0), axis=2)
    chosen = jnp.any(match, axis=2)
    count = chosen.astype(jnp.int32)
    rank = jnp.cumsum(count, axis=-1) - count
    slot = jnp.arange(CAP, dtype=jnp.int32)
    hot = chosen[:, :, None, :] & (rank[:, :, None, :] == slot[None, None, :, None])
    same = jnp.eye(RING, dtype=jnp.bool_)
    block = hot[:, :, :, None, :] & same[None, :, None, :, None]
    pick = block.astype(jnp.bfloat16).reshape(NX * RING * CAP, RING * tok)
    high = lax.reduce_precision(weight, 8, 7)
    low = weight - high
    parts = []
    for part in (high, low):
        spread = jnp.where(block, part[:, :, None, None, :], 0.0).astype(jnp.bfloat16)
        parts.append(spread.reshape(NX * RING * CAP, RING * tok))
    return pick, parts


def picked(plan, normed):
    width = normed.shape[-1]
    rows = jnp.dot(plan[0], normed.reshape(-1, width), preferred_element_type=jnp.float32)
    return rows.astype(jnp.bfloat16).reshape(RING, -1, width)


def expert_rows(rows, gate_local, up_local, down_local):
    blocks, count, width = rows.shape
    rows = rows.reshape(-1, width)
    gate_act = jnp.dot(rows, gate_local, preferred_element_type=jnp.float32)
    up_act = jnp.dot(rows, up_local, preferred_element_type=jnp.float32)
    activated = (jax.nn.silu(gate_act) * up_act).astype(jnp.bfloat16)
    out = jnp.dot(activated, down_local, preferred_element_type=jnp.float32)
    return out.astype(jnp.bfloat16).reshape(blocks, count, width)


def combined(plan, back):
    width = back.shape[-1]
    back = back.reshape(-1, width)
    dims = (((0,), (0,)), ((), ()))
    moe = sum(
        lax.dot_general(part, back, dims, preferred_element_type=jnp.float32) for part in plan[1]
    )
    return moe.astype(jnp.bfloat16).reshape(RING, -1, width)


def finished(hidden, partial):
    moe = jnp.sum(partial.astype(jnp.float32), axis=0)
    return (hidden.astype(jnp.float32) + moe).astype(jnp.bfloat16)


X_THERE = (("x", "swap"),)
X_BACK = (("x", "back"),)
Z_BACK = (("z", "back"),)
START = (("z", "gather"), ("z", "gather"))
GATHER = (("x", "back"), ("z", "gather"))
RETURN = (("x", "swap"), ("z", "back"))


def body(
    fwd_state,
    rev_state,
    norm_gain,
    gate_weight,
    up_weight,
    down_weight,
    fwd_routes,
    rev_routes,
    fwd_combine,
    rev_combine,
):
    index = lax.axis_index("expert")
    x_index = index // NZ
    half = (index % NZ) // (NZ // 2)
    gain_row = norm_gain[0]
    gate, up, down = gate_weight[0], up_weight[0], down_weight[0]
    weights = (
        jnp.concatenate([gate, from_partner(gate)], axis=1),
        jnp.concatenate([up, from_partner(up)], axis=1),
        jnp.concatenate([down, from_partner(down)], axis=0),
    )
    tok = fwd_state.shape[1]
    tables = [a[:, 0].astype(jnp.float32) for a in (fwd_routes, rev_routes, fwd_combine, rev_combine)]
    table = jnp.stack(tables).transpose(0, 1, 3, 2).reshape(-1, tok)
    table = jnp.pad(table, ((0, 0), (0, 128 - tok)))
    fwd, rev = fwd_state[0], rev_state[0]
    fwd_rows, table = exchange(1, START, normed_rows(fwd, gain_row), table)
    table = table[:, :, :tok].reshape(RING, 4, TICKS, 2, tok)

    def plan(stream, tick):
        ids = table[:, stream, tick].astype(jnp.int32)
        return routing(ids, table[:, 2 + stream, tick], x_index, half)

    fwd_plan, rev_plan = plan(0, 0), plan(1, 0)
    (fwd_rows,) = exchange(2, X_THERE, picked(fwd_plan, fwd_rows))
    for tick in range(TICKS):
        fwd_rows, rev_rows = exchange(
            3, GATHER, expert_rows(fwd_rows, *weights), normed_rows(rev, gain_row)
        )
        rev_rows, fwd_rows = exchange(
            4, RETURN, picked(rev_plan, rev_rows), combined(fwd_plan, fwd_rows)
        )
        fwd = finished(fwd, fwd_rows)
        if tick + 1 < TICKS:
            fwd = from_behind(fwd, "pipe", 1)
            fwd_plan = plan(0, tick + 1)
            rev_rows, fwd_rows = exchange(
                3, GATHER, expert_rows(rev_rows, *weights), normed_rows(fwd, gain_row)
            )
            fwd_rows, rev_rows = exchange(
                4, RETURN, picked(fwd_plan, fwd_rows), combined(rev_plan, rev_rows)
            )
            rev = from_behind(finished(rev, rev_rows), "pipe", -1)
            rev_plan = plan(1, tick + 1)
        else:
            (rev_rows,) = exchange(6, X_BACK, expert_rows(rev_rows, *weights))
            (rev_rows,) = exchange(5, Z_BACK, combined(rev_plan, rev_rows))
            rev = finished(rev, rev_rows)
    return (fwd[None], rev[None])


def solution(mesh):
    placed = (
        P("pipe", "expert", None),
        P("pipe", "expert", None),
        P("pipe", None),
        P("pipe", None, "expert"),
        P("pipe", None, "expert"),
        P("pipe", "expert", None),
        P(None, "pipe", "expert", None),
        P(None, "pipe", "expert", None),
        P(None, "pipe", "expert", None),
        P(None, "pipe", "expert", None),
    )
    return jax.shard_map(
        body,
        mesh=mesh,
        in_specs=placed,
        out_specs=(P("pipe", "expert", None), P("pipe", "expert", None)),
        check_vma=False,
    )
```

```python
import functools

import jax
import jax.numpy as jnp
from jax import lax
from jax.experimental import pallas as pl
from jax.experimental.pallas import tpu as pltpu
from jax.sharding import PartitionSpec as P

TICKS = 2
CAP = 24
NX = 4
NZ = 8
RING = 4


def from_behind(block, axis, distance):
    devices = range(lax.axis_size(axis))
    route = [((i - distance) % len(devices), i) for i in devices]
    return lax.ppermute(block, axis, route)


def from_partner(block):
    return lax.ppermute(block, "expert", [(i, i ^ 1) for i in range(NX * NZ)])


def neighbours(axis):
    me = lax.axis_index("expert")
    x, z = me // NZ, me % NZ
    if axis == "x":
        return ((x + 1) % NX) * NZ + z, ((x + NX - 1) % NX) * NZ + z
    return x * NZ + (z + 2) % NZ, x * NZ + (z + NZ - 2) % NZ


def exchange_kernel(jobs, *refs):
    count = len(jobs)
    ins, outs = refs[:count], refs[count : 2 * count]
    relays = refs[2 * count : 3 * count]
    send, recv = refs[3 * count :]
    rings = {axis: neighbours(axis) for axis in dict.fromkeys(axis for axis, _ in jobs)}
    barrier = pltpu.get_barrier_semaphore()
    for pair in rings.values():
        for other in pair:
            pl.semaphore_signal(
                barrier,
                inc=1,
                device_id={"expert": other},
                device_id_type=pl.DeviceIdType.MESH,
            )
    pl.semaphore_wait(barrier, 2 * len(rings))

    def copy(job, number, src, dst, way):
        return pltpu.make_async_remote_copy(
            src_ref=src,
            dst_ref=dst,
            send_sem=send.at[job, number],
            recv_sem=recv.at[job, number],
            device_id={"expert": rings[jobs[job][0]][way]},
            device_id_type=pl.DeviceIdType.MESH,
        )

    first, later, direct = [], [], []
    for job, (_, kind) in enumerate(jobs):
        src, dst, relay = ins[job], outs[job], relays[job]
        rows = dst.shape[1]
        low, high = pl.ds(0, rows // 2), pl.ds(rows // 2, rows // 2)
        if kind == "gather":
            first.append(copy(job, 0, src.at[low], dst.at[1, low], 0))
            first.append(copy(job, 1, src.at[high], dst.at[3, high], 1))
            direct.append(copy(job, 2, src.at[high], dst.at[1, high], 0))
            direct.append(copy(job, 3, src.at[low], dst.at[3, low], 1))
            later.append(copy(job, 4, dst.at[1, low], dst.at[2, low], 0))
            later.append(copy(job, 5, dst.at[3, high], dst.at[2, high], 1))
        else:
            there, back = (0, 1) if kind == "swap" else (1, 0)
            first.append(copy(job, 0, src.at[2, low], relay.at[0], 0))
            first.append(copy(job, 1, src.at[2, high], relay.at[1], 1))
            direct.append(copy(job, 2, src.at[1], dst.at[1], there))
            direct.append(copy(job, 3, src.at[3], dst.at[3], back))
            later.append(copy(job, 4, relay.at[0], dst.at[2, low], 0))
            later.append(copy(job, 5, relay.at[1], dst.at[2, high], 1))
    for one in first + direct:
        one.start()
    for job, (_, kind) in enumerate(jobs):
        outs[job][0] = ins[job][...] if kind == "gather" else ins[job][0]
    for early, late in zip(first, later):
        early.wait_recv()
        late.start()
    for one in first:
        one.wait_send()
    for one in direct + later:
        one.wait()


def exchange(number, jobs, *arrays):
    shapes, relays, sent = [], [], 0
    for (_, kind), array in zip(jobs, arrays):
        rows, width = array.shape[-2:]
        shapes.append(jax.ShapeDtypeStruct((RING, rows, width), array.dtype))
        relays.append(pltpu.VMEM((2, rows // 2, width), array.dtype))
        sent += 4 * rows * width * 2
    whole = pl.BlockSpec(memory_space=pltpu.VMEM)
    return pl.pallas_call(
        functools.partial(exchange_kernel, jobs),
        out_shape=shapes,
        in_specs=[whole] * len(jobs),
        out_specs=[whole] * len(jobs),
        scratch_shapes=relays
        + [pltpu.SemaphoreType.DMA((len(jobs), 6)), pltpu.SemaphoreType.DMA((len(jobs), 6))],
        cost_estimate=pl.CostEstimate(flops=0, bytes_accessed=64_000_000, transcendentals=0),
        compiler_params=pltpu.CompilerParams(collective_id=number, has_side_effects=True),
    )(*arrays)


def normed_rows(hidden, gain_row):
    widened = hidden.astype(jnp.float32)
    scale_inv = lax.rsqrt(jnp.mean(widened * widened, axis=-1, keepdims=True) + 1e-06)
    return (widened * scale_inv * gain_row).astype(jnp.bfloat16)


def routing(ids, weights, x_index, half):
    tok = ids.shape[-1]
    wanted = 2 * ((x_index + jnp.arange(NX, dtype=jnp.int32)) % NX) + half
    match = ids[None] == wanted[:, None, None, None]
    weight = jnp.sum(jnp.where(match, weights[None], 0.0), axis=2)
    chosen = jnp.any(match, axis=2)
    count = chosen.astype(jnp.int32)
    rank = jnp.cumsum(count, axis=-1) - count
    slot = jnp.arange(CAP, dtype=jnp.int32)
    hot = chosen[:, :, None, :] & (rank[:, :, None, :] == slot[None, None, :, None])
    same = jnp.eye(RING, dtype=jnp.bool_)
    block = hot[:, :, :, None, :] & same[None, :, None, :, None]
    pick = block.astype(jnp.bfloat16).reshape(NX * RING * CAP, RING * tok)
    high = lax.reduce_precision(weight, 8, 7)
    low = weight - high
    parts = []
    for part in (high, low):
        spread = jnp.where(block, part[:, :, None, None, :], 0.0).astype(jnp.bfloat16)
        parts.append(spread.reshape(NX * RING * CAP, RING * tok))
    return pick, parts


def picked(plan, normed):
    width = normed.shape[-1]
    rows = jnp.dot(plan[0], normed.reshape(-1, width), preferred_element_type=jnp.float32)
    return rows.astype(jnp.bfloat16).reshape(RING, -1, width)


def expert_rows(rows, gate_up, down):
    blocks, count, width = rows.shape
    rows = rows.reshape(-1, width)
    dims = (((1,), (1,)), ((), ()))
    hidden = lax.dot_general(rows, gate_up, dims, preferred_element_type=jnp.float32)
    units = down.shape[0]
    activated = (jax.nn.silu(hidden[:, :units]) * hidden[:, units:]).astype(jnp.bfloat16)
    out = jnp.dot(activated, down, preferred_element_type=jnp.float32)
    return out.astype(jnp.bfloat16).reshape(blocks, count, width)


def combined(plan, back):
    width = back.shape[-1]
    back = back.reshape(-1, width)
    dims = (((0,), (0,)), ((), ()))
    moe = sum(
        lax.dot_general(part, back, dims, preferred_element_type=jnp.float32) for part in plan[1]
    )
    return moe.astype(jnp.bfloat16).reshape(RING, -1, width)


def finished(hidden, partial):
    moe = jnp.sum(partial.astype(jnp.float32), axis=0)
    return (hidden.astype(jnp.float32) + moe).astype(jnp.bfloat16)


X_THERE = (("x", "swap"),)
X_BACK = (("x", "back"),)
Z_BACK = (("z", "back"),)
START = (("z", "gather"), ("z", "gather"))
GATHER = (("x", "back"), ("z", "gather"))
RETURN = (("x", "swap"), ("z", "back"))


def body(
    fwd_state,
    rev_state,
    norm_gain,
    gate_weight,
    up_weight,
    down_weight,
    fwd_routes,
    rev_routes,
    fwd_combine,
    rev_combine,
):
    index = lax.axis_index("expert")
    x_index = index // NZ
    half = (index % NZ) // (NZ // 2)
    gain_row = norm_gain[0]
    tok = fwd_state.shape[1]
    tables = [a[:, 0].astype(jnp.float32) for a in (fwd_routes, rev_routes, fwd_combine, rev_combine)]
    table = jnp.stack(tables).transpose(0, 1, 3, 2).reshape(-1, tok)
    table = jnp.pad(table, ((0, 0), (0, 128 - tok)))
    fwd, rev = fwd_state[0], rev_state[0]
    fwd_rows, table = exchange(1, START, normed_rows(fwd, gain_row), table)
    mine = jnp.concatenate([gate_weight[0].T, up_weight[0].T, down_weight[0]])
    mine, fwd_rows, table = lax.optimization_barrier((mine, fwd_rows, table))
    part = mine.shape[0] // 3
    other = from_partner(mine)
    both = jnp.stack([mine.reshape(3, part, -1), other.reshape(3, part, -1)], axis=1)
    weights = lax.optimization_barrier(both.reshape(3, 2 * part, -1))
    weights = (weights[:2].reshape(4 * part, -1), weights[2])
    table = table[:, :, :tok].reshape(RING, 4, TICKS, 2, tok)

    def plan(stream, tick):
        ids = table[:, stream, tick].astype(jnp.int32)
        return routing(ids, table[:, 2 + stream, tick], x_index, half)

    fwd_plan, rev_plan = plan(0, 0), plan(1, 0)
    (fwd_rows,) = exchange(2, X_THERE, picked(fwd_plan, fwd_rows))
    for tick in range(TICKS):
        fwd_rows, rev_rows = exchange(
            3, GATHER, expert_rows(fwd_rows, *weights), normed_rows(rev, gain_row)
        )
        rev_rows, fwd_rows = exchange(
            4, RETURN, picked(rev_plan, rev_rows), combined(fwd_plan, fwd_rows)
        )
        fwd = finished(fwd, fwd_rows)
        if tick + 1 < TICKS:
            fwd = from_behind(fwd, "pipe", 1)
            fwd_plan = plan(0, tick + 1)
            rev_rows, fwd_rows = exchange(
                3, GATHER, expert_rows(rev_rows, *weights), normed_rows(fwd, gain_row)
            )
            fwd_rows, rev_rows = exchange(
                4, RETURN, picked(fwd_plan, fwd_rows), combined(rev_plan, rev_rows)
            )
            rev = from_behind(finished(rev, rev_rows), "pipe", -1)
            rev_plan = plan(1, tick + 1)
        else:
            (rev_rows,) = exchange(6, X_BACK, expert_rows(rev_rows, *weights))
            (rev_rows,) = exchange(5, Z_BACK, combined(rev_plan, rev_rows))
            rev = finished(rev, rev_rows)
    return (fwd[None], rev[None])


def solution(mesh):
    placed = (
        P("pipe", "expert", None),
        P("pipe", "expert", None),
        P("pipe", None),
        P("pipe", None, "expert"),
        P("pipe", None, "expert"),
        P("pipe", "expert", None),
        P(None, "pipe", "expert", None),
        P(None, "pipe", "expert", None),
        P(None, "pipe", "expert", None),
        P(None, "pipe", "expert", None),
    )
    return jax.shard_map(
        body,
        mesh=mesh,
        in_specs=placed,
        out_specs=(P("pipe", "expert", None), P("pipe", "expert", None)),
        check_vma=False,
    )
```

```python
import functools

import jax
import jax.numpy as jnp
from jax import lax
from jax.experimental import pallas as pl
from jax.experimental.pallas import tpu as pltpu
from jax.sharding import PartitionSpec as P

TICKS = 2
CAP = 24
NX = 4
NZ = 8
RING = 4


def from_behind(block, axis, distance):
    devices = range(lax.axis_size(axis))
    route = [((i - distance) % len(devices), i) for i in devices]
    return lax.ppermute(block, axis, route)


def from_partner(block):
    return lax.ppermute(block, "expert", [(i, i ^ 1) for i in range(NX * NZ)])


def neighbours(axis):
    me = lax.axis_index("expert")
    x, z = me // NZ, me % NZ
    if axis == "x":
        return ((x + 1) % NX) * NZ + z, ((x + NX - 1) % NX) * NZ + z
    return x * NZ + (z + 2) % NZ, x * NZ + (z + NZ - 2) % NZ


def exchange_kernel(jobs, *refs):
    count = len(jobs)
    ins, outs = refs[:count], refs[count : 2 * count]
    relays, owns = refs[2 * count : 3 * count], refs[3 * count : 4 * count]
    send, recv, local = refs[4 * count :]
    rings = {axis: neighbours(axis) for axis in dict.fromkeys(axis for axis, _ in jobs)}
    first, later, direct, loads, stores = [], [], [], [], []

    def copy(job, number, src, dst, way):
        return pltpu.make_async_remote_copy(
            src_ref=src,
            dst_ref=dst,
            send_sem=send.at[job, number],
            recv_sem=recv.at[job, number],
            device_id={"expert": rings[jobs[job][0]][way]},
            device_id_type=pl.DeviceIdType.MESH,
        )

    for job, (_, kind) in enumerate(jobs):
        src, dst, relay, own = ins[job], outs[job], relays[job], owns[job]
        rows = dst.shape[1]
        low, high = pl.ds(0, rows // 2), pl.ds(rows // 2, rows // 2)
        if kind == "gather":
            first.append(copy(job, 0, src.at[low], dst.at[1, low], 0))
            first.append(copy(job, 1, src.at[high], dst.at[3, high], 1))
            direct.append(copy(job, 2, src.at[high], dst.at[1, high], 0))
            direct.append(copy(job, 3, src.at[low], dst.at[3, low], 1))
            later.append(copy(job, 4, dst.at[1, low], dst.at[2, low], 0))
            later.append(copy(job, 5, dst.at[3, high], dst.at[2, high], 1))
            loads.append([(src, own)])
        elif kind == "reduce":
            first.append(copy(job, 0, src.at[2, low], relay.at[0], 0))
            first.append(copy(job, 1, src.at[2, high], relay.at[1], 1))
            direct.append(copy(job, 2, src.at[3, high], dst.at[0, high], 0))
            direct.append(copy(job, 3, src.at[1, low], dst.at[1, low], 1))
            later.append(copy(job, 4, relay.at[0], dst.at[0, low], 0))
            later.append(copy(job, 5, relay.at[1], dst.at[1, high], 1))
            loads.append([(src.at[3, low], own.at[low]), (src.at[1, high], own.at[high])])
        else:
            there, back = (0, 1) if kind == "swap" else (1, 0)
            first.append(copy(job, 0, src.at[2, low], relay.at[0], 0))
            first.append(copy(job, 1, src.at[2, high], relay.at[1], 1))
            direct.append(copy(job, 2, src.at[1], dst.at[1], there))
            direct.append(copy(job, 3, src.at[3], dst.at[3], back))
            later.append(copy(job, 4, relay.at[0], dst.at[2, low], 0))
            later.append(copy(job, 5, relay.at[1], dst.at[2, high], 1))
            loads.append([(src.at[0], own)])
        loads[job] = [
            pltpu.make_async_copy(one, two, local.at[job, number])
            for number, (one, two) in enumerate(loads[job])
        ]
        for load in loads[job]:
            load.start()

    barrier = pltpu.get_barrier_semaphore()
    for pair in rings.values():
        for other in pair:
            pl.semaphore_signal(
                barrier,
                inc=1,
                device_id={"expert": other},
                device_id_type=pl.DeviceIdType.MESH,
            )
    pl.semaphore_wait(barrier, 2 * len(rings))
    for one in first + direct:
        one.start()
    for job, (_, kind) in enumerate(jobs):
        for load in loads[job]:
            load.wait()
        if kind != "reduce":
            stores.append(pltpu.make_async_copy(owns[job], outs[job].at[0], local.at[job, 2]))
            stores[-1].start()
    for number, (early, late) in enumerate(zip(first, later)):
        early.wait_recv()
        job, part = number // 2, number % 2
        if jobs[job][1] == "reduce":
            relay, rows = relays[job], owns[job].shape[0] // 2
            mine = owns[job][pl.ds(part * rows, rows)]
            total = relay[part].astype(jnp.float32) + mine.astype(jnp.float32)
            relay[part] = total.astype(relay.dtype)
        late.start()
    for one in first:
        one.wait_send()
    for one in direct + later + stores:
        one.wait()


def exchange(number, jobs, *arrays):
    shapes, relays, owns = [], [], []
    for (_, kind), array in zip(jobs, arrays):
        rows, width = array.shape[-2:]
        blocks = 2 if kind == "reduce" else RING
        shapes.append(jax.ShapeDtypeStruct((blocks, rows, width), array.dtype))
        relays.append(pltpu.VMEM((2, rows // 2, width), array.dtype))
        owns.append(pltpu.VMEM((rows, width), array.dtype))
    anywhere = pl.BlockSpec(memory_space=pl.ANY)
    return pl.pallas_call(
        functools.partial(exchange_kernel, jobs),
        out_shape=shapes,
        in_specs=[anywhere] * len(jobs),
        out_specs=[anywhere] * len(jobs),
        scratch_shapes=relays
        + owns
        + [pltpu.SemaphoreType.DMA((len(jobs), 6))] * 2
        + [pltpu.SemaphoreType.DMA((len(jobs), 3))],
        cost_estimate=pl.CostEstimate(flops=0, bytes_accessed=64_000_000, transcendentals=0),
        compiler_params=pltpu.CompilerParams(
            collective_id=number, has_side_effects=True, vmem_limit_bytes=8 * 1024 * 1024
        ),
    )(*arrays)


def normed_rows(hidden, gain_row):
    widened = hidden.astype(jnp.float32)
    scale_inv = lax.rsqrt(jnp.mean(widened * widened, axis=-1, keepdims=True) + 1e-06)
    return (widened * scale_inv * gain_row).astype(jnp.bfloat16)


def routing(ids, weights, x_index, half):
    tok = ids.shape[-1]
    wanted = 2 * ((x_index + jnp.arange(NX, dtype=jnp.int32)) % NX) + half
    match = ids[None] == wanted[:, None, None, None]
    weight = jnp.sum(jnp.where(match, weights[None], 0.0), axis=2)
    chosen = jnp.any(match, axis=2)
    count = chosen.astype(jnp.int32)
    rank = jnp.cumsum(count, axis=-1) - count
    slot = jnp.arange(CAP, dtype=jnp.int32)
    hot = chosen[:, :, None, :] & (rank[:, :, None, :] == slot[None, None, :, None])
    same = jnp.eye(RING, dtype=jnp.bool_)
    block = hot[:, :, :, None, :] & same[None, :, None, :, None]
    pick = block.astype(jnp.bfloat16).reshape(NX * RING * CAP, RING * tok)
    high = lax.reduce_precision(weight, 8, 7)
    low = weight - high
    parts = []
    for part in (high, low):
        spread = jnp.where(block, part[:, :, None, None, :], 0.0).astype(jnp.bfloat16)
        parts.append(spread.reshape(NX * RING * CAP, RING * tok))
    return pick, parts


def picked(plan, normed):
    width = normed.shape[-1]
    rows = jnp.dot(plan[0], normed.reshape(-1, width), preferred_element_type=jnp.float32)
    return rows.astype(jnp.bfloat16).reshape(RING, -1, width)


def expert_rows(rows, gate_up, down):
    blocks, count, width = rows.shape
    rows = rows.reshape(-1, width)
    dims = (((1,), (1,)), ((), ()))
    hidden = lax.dot_general(rows, gate_up, dims, preferred_element_type=jnp.float32)
    units = down.shape[0]
    activated = (jax.nn.silu(hidden[:, :units]) * hidden[:, units:]).astype(jnp.bfloat16)
    out = jnp.dot(activated, down, preferred_element_type=jnp.float32)
    return out.astype(jnp.bfloat16).reshape(blocks, count, width)


def combined(plan, back):
    width = back.shape[-1]
    back = back.reshape(-1, width)
    dims = (((0,), (0,)), ((), ()))
    moe = sum(
        lax.dot_general(part, back, dims, preferred_element_type=jnp.float32) for part in plan[1]
    )
    return moe.astype(jnp.bfloat16).reshape(RING, -1, width)


def finished(hidden, own, partial):
    moe = jnp.sum(partial.astype(jnp.float32), axis=0) + own[0].astype(jnp.float32)
    return (hidden.astype(jnp.float32) + moe).astype(jnp.bfloat16)


X_THERE = (("x", "swap"),)
X_BACK = (("x", "back"),)
Z_BACK = (("z", "reduce"),)
START = (("z", "gather"), ("z", "gather"))
GATHER = (("x", "back"), ("z", "gather"))
RETURN = (("x", "swap"), ("z", "reduce"))


def body(
    fwd_state,
    rev_state,
    norm_gain,
    gate_weight,
    up_weight,
    down_weight,
    fwd_routes,
    rev_routes,
    fwd_combine,
    rev_combine,
):
    index = lax.axis_index("expert")
    x_index = index // NZ
    half = (index % NZ) // (NZ // 2)
    gain_row = norm_gain[0]
    tok = fwd_state.shape[1]
    tables = [a[:, 0].astype(jnp.float32) for a in (fwd_routes, rev_routes, fwd_combine, rev_combine)]
    table = jnp.stack(tables).transpose(0, 1, 3, 2).reshape(-1, tok)
    table = jnp.pad(table, ((0, 0), (0, 128 - tok)))
    fwd, rev = fwd_state[0], rev_state[0]
    fwd_rows, table = exchange(1, START, normed_rows(fwd, gain_row), table)
    mine = jnp.concatenate([gate_weight[0].T, up_weight[0].T, down_weight[0]])
    mine, fwd_rows, table = lax.optimization_barrier((mine, fwd_rows, table))
    part = mine.shape[0] // 3
    other = from_partner(mine)
    both = jnp.stack([mine.reshape(3, part, -1), other.reshape(3, part, -1)], axis=1)
    weights = lax.optimization_barrier(both.reshape(3, 2 * part, -1))
    weights = (weights[:2].reshape(4 * part, -1), weights[2])
    table = table[:, :, :tok].reshape(RING, 4, TICKS, 2, tok)

    def plan(stream, tick):
        ids = table[:, stream, tick].astype(jnp.int32)
        return routing(ids, table[:, 2 + stream, tick], x_index, half)

    fwd_plan, rev_plan = plan(0, 0), plan(1, 0)
    (fwd_rows,) = exchange(2, X_THERE, picked(fwd_plan, fwd_rows))
    for tick in range(TICKS):
        fwd_rows, rev_rows = exchange(
            3, GATHER, expert_rows(fwd_rows, *weights), normed_rows(rev, gain_row)
        )
        own = combined(fwd_plan, fwd_rows)
        rev_rows, fwd_rows = exchange(4, RETURN, picked(rev_plan, rev_rows), own)
        fwd = finished(fwd, own, fwd_rows)
        if tick + 1 < TICKS:
            fwd = from_behind(fwd, "pipe", 1)
            fwd_plan = plan(0, tick + 1)
            rev_rows, fwd_rows = exchange(
                3, GATHER, expert_rows(rev_rows, *weights), normed_rows(fwd, gain_row)
            )
            own = combined(rev_plan, rev_rows)
            fwd_rows, rev_rows = exchange(4, RETURN, picked(fwd_plan, fwd_rows), own)
            rev = from_behind(finished(rev, own, rev_rows), "pipe", -1)
            rev_plan = plan(1, tick + 1)
        else:
            (rev_rows,) = exchange(6, X_BACK, expert_rows(rev_rows, *weights))
            own = combined(rev_plan, rev_rows)
            (rev_rows,) = exchange(5, Z_BACK, own)
            rev = finished(rev, own, rev_rows)
    return (fwd[None], rev[None])


def solution(mesh):
    placed = (
        P("pipe", "expert", None),
        P("pipe", "expert", None),
        P("pipe", None),
        P("pipe", None, "expert"),
        P("pipe", None, "expert"),
        P("pipe", "expert", None),
        P(None, "pipe", "expert", None),
        P(None, "pipe", "expert", None),
        P(None, "pipe", "expert", None),
        P(None, "pipe", "expert", None),
    )
    return jax.shard_map(
        body,
        mesh=mesh,
        in_specs=placed,
        out_specs=(P("pipe", "expert", None), P("pipe", "expert", None)),
        check_vma=False,
    )
```

```python
import functools

import jax
import jax.numpy as jnp
from jax import lax
from jax.experimental import pallas as pl
from jax.experimental.pallas import tpu as pltpu
from jax.sharding import PartitionSpec as P

TICKS = 2
CAP = 24
NX = 4
NZ = 8
RING = 4


def from_partner(block):
    return lax.ppermute(block, "expert", [(i, i ^ 1) for i in range(NX * NZ)])


def neighbours(axis):
    me = lax.axis_index("expert")
    x, z = me // NZ, me % NZ
    if axis == "x":
        return ((x + 1) % NX) * NZ + z, ((x + NX - 1) % NX) * NZ + z
    return x * NZ + (z + 2) % NZ, x * NZ + (z + NZ - 2) % NZ


def exchange_kernel(jobs, shift, *refs):
    count = len(jobs)
    if shift:
        hidden, carry = refs[count], refs[2 * count + 1]
        refs = refs[:count] + refs[count + 1 : 2 * count + 1] + refs[2 * count + 2 :]
    ins, outs = refs[:count], refs[count : 2 * count]
    relays, owns = refs[2 * count : 3 * count], refs[3 * count : 4 * count]
    send, recv, local = refs[4 * count :]
    me, section, sections = lax.axis_index("expert"), lax.axis_index("pipe"), lax.axis_size("pipe")
    onward = (section + sections + shift) % sections
    behind = (section + sections - shift) % sections
    rings = {axis: neighbours(axis) for axis in dict.fromkeys(axis for axis, _ in jobs)}
    first, later, direct, loads, stores = [], [], [], [], []

    def remote(job, number, src, dst, device):
        return pltpu.make_async_remote_copy(
            src_ref=src,
            dst_ref=dst,
            send_sem=send.at[job, number],
            recv_sem=recv.at[job, number],
            device_id=device,
            device_id_type=pl.DeviceIdType.MESH,
        )

    def copy(job, number, src, dst, way):
        return remote(job, number, src, dst, {"expert": rings[jobs[job][0]][way]})

    def last(job, number, src, dst, way):
        target = {"expert": rings[jobs[job][0]][way], "pipe": onward if shift else section}
        return remote(job, number, src, dst, target)

    for job, (_, kind) in enumerate(jobs):
        src, dst, relay, own = ins[job], outs[job], relays[job], owns[job]
        rows = dst.shape[1]
        low, high = pl.ds(0, rows // 2), pl.ds(rows // 2, rows // 2)
        if kind == "gather":
            first.append(copy(job, 0, src.at[low], dst.at[1, low], 0))
            first.append(copy(job, 1, src.at[high], dst.at[3, high], 1))
            direct.append(copy(job, 2, src.at[high], dst.at[1, high], 0))
            direct.append(copy(job, 3, src.at[low], dst.at[3, low], 1))
            later.append(copy(job, 4, dst.at[1, low], dst.at[2, low], 0))
            later.append(copy(job, 5, dst.at[3, high], dst.at[2, high], 1))
            loads.append([(src, own)])
        elif kind == "reduce":
            first.append(copy(job, 0, src.at[2, low], relay.at[0], 0))
            first.append(copy(job, 1, src.at[2, high], relay.at[1], 1))
            direct.append(last(job, 2, src.at[3, high], dst.at[0, high], 0))
            direct.append(last(job, 3, src.at[1, low], dst.at[1, low], 1))
            later.append(last(job, 4, relay.at[0], dst.at[0, low], 0))
            later.append(last(job, 5, relay.at[1], dst.at[1, high], 1))
            if shift:
                ahead = {"expert": me, "pipe": onward}
                direct.append(remote(job, 6, hidden, carry.at[0], ahead))
                direct.append(remote(job, 7, src.at[0], carry.at[1], ahead))
            loads.append([(src.at[3, low], own.at[low]), (src.at[1, high], own.at[high])])
        else:
            there, back = (0, 1) if kind == "swap" else (1, 0)
            first.append(copy(job, 0, src.at[2, low], relay.at[0], 0))
            first.append(copy(job, 1, src.at[2, high], relay.at[1], 1))
            direct.append(copy(job, 2, src.at[1], dst.at[1], there))
            direct.append(copy(job, 3, src.at[3], dst.at[3], back))
            later.append(copy(job, 4, relay.at[0], dst.at[2, low], 0))
            later.append(copy(job, 5, relay.at[1], dst.at[2, high], 1))
            loads.append([(src.at[0], own)])
        loads[job] = [
            pltpu.make_async_copy(one, two, local.at[job, number])
            for number, (one, two) in enumerate(loads[job])
        ]
        for load in loads[job]:
            load.start()

    barrier = pltpu.get_barrier_semaphore()
    for pair in rings.values():
        for other in pair:
            pl.semaphore_signal(
                barrier,
                inc=1,
                device_id={"expert": other},
                device_id_type=pl.DeviceIdType.MESH,
            )
    greeted = 2 * len(rings)
    if shift:
        for other in (me, *rings["z"]):
            pl.semaphore_signal(
                barrier,
                inc=1,
                device_id={"expert": other, "pipe": behind},
                device_id_type=pl.DeviceIdType.MESH,
            )
        greeted += 3
    pl.semaphore_wait(barrier, greeted)
    for one in first + direct:
        one.start()
    for job, (_, kind) in enumerate(jobs):
        for load in loads[job]:
            load.wait()
        if kind != "reduce":
            stores.append(pltpu.make_async_copy(owns[job], outs[job].at[0], local.at[job, 2]))
            stores[-1].start()
    for number, (early, late) in enumerate(zip(first, later)):
        early.wait_recv()
        job, part = number // 2, number % 2
        if jobs[job][1] == "reduce":
            relay, rows = relays[job], owns[job].shape[0] // 2
            mine = owns[job][pl.ds(part * rows, rows)]
            total = relay[part].astype(jnp.float32) + mine.astype(jnp.float32)
            relay[part] = total.astype(relay.dtype)
        late.start()
    for one in first:
        one.wait_send()
    for one in direct + later + stores:
        one.wait()


def exchange(number, jobs, *arrays, shift=0):
    shapes, relays, owns = [], [], []
    for (_, kind), array in zip(jobs, arrays):
        rows, width = array.shape[-2:]
        blocks = 2 if kind == "reduce" else RING
        shapes.append(jax.ShapeDtypeStruct((blocks, rows, width), array.dtype))
        relays.append(pltpu.VMEM((2, rows // 2, width), array.dtype))
        owns.append(pltpu.VMEM((rows, width), array.dtype))
    if shift:
        shapes.append(jax.ShapeDtypeStruct((2,) + arrays[-1].shape, arrays[-1].dtype))
    anywhere = pl.BlockSpec(memory_space=pl.ANY)
    return pl.pallas_call(
        functools.partial(exchange_kernel, jobs, shift),
        out_shape=shapes,
        in_specs=[anywhere] * len(arrays),
        out_specs=[anywhere] * len(shapes),
        scratch_shapes=relays
        + owns
        + [pltpu.SemaphoreType.DMA((len(jobs), 8))] * 2
        + [pltpu.SemaphoreType.DMA((len(jobs), 3))],
        cost_estimate=pl.CostEstimate(flops=0, bytes_accessed=64_000_000, transcendentals=0),
        compiler_params=pltpu.CompilerParams(
            collective_id=number, has_side_effects=True, vmem_limit_bytes=8 * 1024 * 1024
        ),
    )(*arrays)


def normed_rows(hidden, gain_row):
    widened = hidden.astype(jnp.float32)
    scale_inv = lax.rsqrt(jnp.mean(widened * widened, axis=-1, keepdims=True) + 1e-06)
    return (widened * scale_inv * gain_row).astype(jnp.bfloat16)


def routing(ids, weights, x_index, half):
    tok = ids.shape[-1]
    wanted = 2 * ((x_index + jnp.arange(NX, dtype=jnp.int32)) % NX) + half
    match = ids[None] == wanted[:, None, None, None]
    weight = jnp.sum(jnp.where(match, weights[None], 0.0), axis=2)
    chosen = jnp.any(match, axis=2)
    count = chosen.astype(jnp.int32)
    rank = jnp.cumsum(count, axis=-1) - count
    slot = jnp.arange(CAP, dtype=jnp.int32)
    hot = chosen[:, :, None, :] & (rank[:, :, None, :] == slot[None, None, :, None])
    same = jnp.eye(RING, dtype=jnp.bool_)
    block = hot[:, :, :, None, :] & same[None, :, None, :, None]
    pick = block.astype(jnp.bfloat16).reshape(NX * RING * CAP, RING * tok)
    high = lax.reduce_precision(weight, 8, 7)
    low = weight - high
    parts = []
    for part in (high, low):
        spread = jnp.where(block, part[:, :, None, None, :], 0.0).astype(jnp.bfloat16)
        parts.append(spread.reshape(NX * RING * CAP, RING * tok))
    return pick, parts


def picked(plan, normed):
    width = normed.shape[-1]
    rows = jnp.dot(plan[0], normed.reshape(-1, width), preferred_element_type=jnp.float32)
    return rows.astype(jnp.bfloat16).reshape(RING, -1, width)


def expert_rows(rows, gate_up, down):
    blocks, count, width = rows.shape
    rows = rows.reshape(-1, width)
    dims = (((1,), (1,)), ((), ()))
    hidden = lax.dot_general(rows, gate_up, dims, preferred_element_type=jnp.float32)
    units = down.shape[0]
    activated = (jax.nn.silu(hidden[:, :units]) * hidden[:, units:]).astype(jnp.bfloat16)
    out = jnp.dot(activated, down, preferred_element_type=jnp.float32)
    return out.astype(jnp.bfloat16).reshape(blocks, count, width)


def combined(plan, back):
    width = back.shape[-1]
    back = back.reshape(-1, width)
    dims = (((0,), (0,)), ((), ()))
    moe = sum(
        lax.dot_general(part, back, dims, preferred_element_type=jnp.float32) for part in plan[1]
    )
    return moe.astype(jnp.bfloat16).reshape(RING, -1, width)


def finished(hidden, own, partial):
    moe = jnp.sum(partial.astype(jnp.float32), axis=0) + own[0].astype(jnp.float32)
    return (hidden.astype(jnp.float32) + moe).astype(jnp.bfloat16)


X_THERE = (("x", "swap"),)
X_BACK = (("x", "back"),)
Z_BACK = (("z", "reduce"),)
START = (("z", "gather"), ("z", "gather"))
GATHER = (("x", "back"), ("z", "gather"))
RETURN = (("x", "swap"), ("z", "reduce"))


def body(
    fwd_state,
    rev_state,
    norm_gain,
    gate_weight,
    up_weight,
    down_weight,
    fwd_routes,
    rev_routes,
    fwd_combine,
    rev_combine,
):
    index = lax.axis_index("expert")
    x_index = index // NZ
    half = (index % NZ) // (NZ // 2)
    gain_row = norm_gain[0]
    tok = fwd_state.shape[1]
    tables = [a[:, 0].astype(jnp.float32) for a in (fwd_routes, rev_routes, fwd_combine, rev_combine)]
    table = jnp.stack(tables).transpose(0, 1, 3, 2).reshape(-1, tok)
    table = jnp.pad(table, ((0, 0), (0, 128 - tok)))
    fwd, rev = fwd_state[0], rev_state[0]
    fwd_rows, table = exchange(1, START, normed_rows(fwd, gain_row), table)
    mine = (gate_weight[0].T, up_weight[0].T, down_weight[0])
    mine, fwd_rows, table = lax.optimization_barrier((mine, fwd_rows, table))
    gate, up, down = [(one, from_partner(one)) for one in mine]
    weights = lax.optimization_barrier((jnp.concatenate(gate + up), jnp.concatenate(down)))
    table = table[:, :, :tok].reshape(RING, 4, TICKS, 2, tok)

    def plan(stream, tick):
        ids = table[:, stream, tick].astype(jnp.int32)
        return routing(ids, table[:, 2 + stream, tick], x_index, half)

    fwd_plan, rev_plan = plan(0, 0), plan(1, 0)
    (fwd_rows,) = exchange(2, X_THERE, picked(fwd_plan, fwd_rows))
    for tick in range(TICKS):
        fwd_rows, rev_rows = exchange(
            3, GATHER, expert_rows(fwd_rows, *weights), normed_rows(rev, gain_row)
        )
        own = combined(fwd_plan, fwd_rows)
        rows = picked(rev_plan, rev_rows)
        if tick + 1 < TICKS:
            rev_rows, fwd_rows, carry = exchange(7, RETURN, rows, own, fwd, shift=1)
            fwd = finished(carry[0], carry[1:], fwd_rows)
            fwd_plan = plan(0, tick + 1)
            rev_rows, fwd_rows = exchange(
                3, GATHER, expert_rows(rev_rows, *weights), normed_rows(fwd, gain_row)
            )
            own = combined(rev_plan, rev_rows)
            rows = picked(fwd_plan, fwd_rows)
            fwd_rows, rev_rows, carry = exchange(8, RETURN, rows, own, rev, shift=-1)
            rev = finished(carry[0], carry[1:], rev_rows)
            rev_plan = plan(1, tick + 1)
        else:
            rev_rows, fwd_rows = exchange(4, RETURN, rows, own)
            fwd = finished(fwd, own, fwd_rows)
            (rev_rows,) = exchange(6, X_BACK, expert_rows(rev_rows, *weights))
            own = combined(rev_plan, rev_rows)
            (rev_rows,) = exchange(5, Z_BACK, own)
            rev = finished(rev, own, rev_rows)
    return (fwd[None], rev[None])


def solution(mesh):
    placed = (
        P("pipe", "expert", None),
        P("pipe", "expert", None),
        P("pipe", None),
        P("pipe", None, "expert"),
        P("pipe", None, "expert"),
        P("pipe", "expert", None),
        P(None, "pipe", "expert", None),
        P(None, "pipe", "expert", None),
        P(None, "pipe", "expert", None),
        P(None, "pipe", "expert", None),
    )
    return jax.shard_map(
        body,
        mesh=mesh,
        in_specs=placed,
        out_specs=(P("pipe", "expert", None), P("pipe", "expert", None)),
        check_vma=False,
    )
```

```python
import functools

import jax
import jax.numpy as jnp
from jax import lax
from jax.experimental import pallas as pl
from jax.experimental.pallas import tpu as pltpu
from jax.sharding import PartitionSpec as P

TICKS = 2
CAP = 24
NX = 4
NZ = 8
RING = 4


def from_partner(block):
    return lax.ppermute(block, "expert", [(i, i ^ 1) for i in range(NX * NZ)])


def neighbours(axis):
    me = lax.axis_index("expert")
    x, z = me // NZ, me % NZ
    if axis == "x":
        return ((x + 1) % NX) * NZ + z, ((x + NX - 1) % NX) * NZ + z
    return x * NZ + (z + 2) % NZ, x * NZ + (z + NZ - 2) % NZ


def exchange_kernel(jobs, shift, *refs):
    count = len(jobs)
    if shift:
        hidden, carry = refs[count], refs[2 * count + 1]
        refs = refs[:count] + refs[count + 1 : 2 * count + 1] + refs[2 * count + 2 :]
    ins, outs = refs[:count], refs[count : 2 * count]
    relays, owns = refs[2 * count : 3 * count], refs[3 * count : 4 * count]
    send, recv, local = refs[4 * count :]
    me, section, sections = lax.axis_index("expert"), lax.axis_index("pipe"), lax.axis_size("pipe")
    onward = (section + sections + shift) % sections
    behind = (section + sections - shift) % sections
    rings = {axis: neighbours(axis) for axis in dict.fromkeys(axis for axis, _ in jobs)}
    first, later, direct, loads, stores = [], [], [], [], []

    def remote(job, number, src, dst, device):
        return pltpu.make_async_remote_copy(
            src_ref=src,
            dst_ref=dst,
            send_sem=send.at[job, number],
            recv_sem=recv.at[job, number],
            device_id=device,
            device_id_type=pl.DeviceIdType.MESH,
        )

    def copy(job, number, src, dst, way):
        return remote(job, number, src, dst, {"expert": rings[jobs[job][0]][way]})

    def last(job, number, src, dst, way):
        target = {"expert": rings[jobs[job][0]][way], "pipe": onward if shift else section}
        return remote(job, number, src, dst, target)

    for job, (_, kind) in enumerate(jobs):
        src, dst, relay, own = ins[job], outs[job], relays[job], owns[job]
        rows = dst.shape[1]
        low, high = pl.ds(0, rows // 2), pl.ds(rows // 2, rows // 2)
        if kind == "gather":
            first.append(copy(job, 0, src.at[low], dst.at[1, low], 0))
            first.append(copy(job, 1, src.at[high], dst.at[3, high], 1))
            direct.append(copy(job, 2, src.at[high], dst.at[1, high], 0))
            direct.append(copy(job, 3, src.at[low], dst.at[3, low], 1))
            later.append(copy(job, 4, dst.at[1, low], dst.at[2, low], 0))
            later.append(copy(job, 5, dst.at[3, high], dst.at[2, high], 1))
            loads.append([(src, own)])
        elif kind == "reduce":
            first.append(copy(job, 0, src.at[2, low], relay.at[0], 0))
            first.append(copy(job, 1, src.at[2, high], relay.at[1], 1))
            direct.append(last(job, 2, src.at[3, high], dst.at[0, high], 0))
            direct.append(last(job, 3, src.at[1, low], dst.at[1, low], 1))
            later.append(last(job, 4, relay.at[0], dst.at[0, low], 0))
            later.append(last(job, 5, relay.at[1], dst.at[1, high], 1))
            if shift:
                ahead = {"expert": me, "pipe": onward}
                direct.append(remote(job, 6, hidden, carry.at[0], ahead))
                direct.append(remote(job, 7, src.at[0], carry.at[1], ahead))
            loads.append([(src.at[3, low], own.at[low]), (src.at[1, high], own.at[high])])
        else:
            there, back = (0, 1) if kind == "swap" else (1, 0)
            first.append(copy(job, 0, src.at[2, low], relay.at[0], 0))
            first.append(copy(job, 1, src.at[2, high], relay.at[1], 1))
            direct.append(copy(job, 2, src.at[1], dst.at[1], there))
            direct.append(copy(job, 3, src.at[3], dst.at[3], back))
            later.append(copy(job, 4, relay.at[0], dst.at[2, low], 0))
            later.append(copy(job, 5, relay.at[1], dst.at[2, high], 1))
            loads.append([(src.at[0], own)])
        loads[job] = [
            pltpu.make_async_copy(one, two, local.at[job, number])
            for number, (one, two) in enumerate(loads[job])
        ]
        for load in loads[job]:
            load.start()

    barrier = pltpu.get_barrier_semaphore()
    for pair in rings.values():
        for other in pair:
            pl.semaphore_signal(
                barrier,
                inc=1,
                device_id={"expert": other},
                device_id_type=pl.DeviceIdType.MESH,
            )
    greeted = 2 * len(rings)
    if shift:
        for other in (me, *rings["z"]):
            pl.semaphore_signal(
                barrier,
                inc=1,
                device_id={"expert": other, "pipe": behind},
                device_id_type=pl.DeviceIdType.MESH,
            )
        greeted += 3
    pl.semaphore_wait(barrier, greeted)
    for one in first + direct:
        one.start()
    for job, (_, kind) in enumerate(jobs):
        for load in loads[job]:
            load.wait()
        if kind != "reduce":
            stores.append(pltpu.make_async_copy(owns[job], outs[job].at[0], local.at[job, 2]))
            stores[-1].start()
    for number, (early, late) in enumerate(zip(first, later)):
        early.wait_recv()
        job, part = number // 2, number % 2
        if jobs[job][1] == "reduce":
            relay, rows = relays[job], owns[job].shape[0] // 2
            mine = owns[job][pl.ds(part * rows, rows)]
            total = relay[part].astype(jnp.float32) + mine.astype(jnp.float32)
            relay[part] = total.astype(relay.dtype)
        late.start()
    for one in first:
        one.wait_send()
    for one in direct + later + stores:
        one.wait()


def exchange(number, jobs, *arrays, shift=0):
    shapes, relays, owns = [], [], []
    for (_, kind), array in zip(jobs, arrays):
        rows, width = array.shape[-2:]
        blocks = 2 if kind == "reduce" else RING
        shapes.append(jax.ShapeDtypeStruct((blocks, rows, width), array.dtype))
        relays.append(pltpu.VMEM((2, rows // 2, width), array.dtype))
        owns.append(pltpu.VMEM((rows, width), array.dtype))
    if shift:
        shapes.append(jax.ShapeDtypeStruct((2,) + arrays[-1].shape, arrays[-1].dtype))
    anywhere = pl.BlockSpec(memory_space=pl.ANY)
    return pl.pallas_call(
        functools.partial(exchange_kernel, jobs, shift),
        out_shape=shapes,
        in_specs=[anywhere] * len(arrays),
        out_specs=[anywhere] * len(shapes),
        scratch_shapes=relays
        + owns
        + [pltpu.SemaphoreType.DMA((len(jobs), 8))] * 2
        + [pltpu.SemaphoreType.DMA((len(jobs), 3))],
        cost_estimate=pl.CostEstimate(flops=0, bytes_accessed=64_000_000, transcendentals=0),
        compiler_params=pltpu.CompilerParams(
            collective_id=number, has_side_effects=True, vmem_limit_bytes=8 * 1024 * 1024
        ),
    )(*arrays)


def normed_rows(hidden, gain_row):
    widened = hidden.astype(jnp.float32)
    scale_inv = lax.rsqrt(jnp.mean(widened * widened, axis=-1, keepdims=True) + 1e-06)
    return (widened * scale_inv * gain_row).astype(jnp.bfloat16)


def routing(ids, weights, x_index, half):
    tok = ids.shape[-1]
    wanted = 2 * ((x_index + jnp.arange(NX, dtype=jnp.int32)) % NX) + half
    match = ids[None] == wanted[:, None, None, None]
    weight = jnp.sum(jnp.where(match, weights[None], 0.0), axis=2)
    chosen = jnp.any(match, axis=2)
    count = chosen.astype(jnp.int32)
    rank = jnp.cumsum(count, axis=-1) - count
    lanes = RING * tok
    rank = jnp.where(chosen, rank, -1).reshape(NX, 1, lanes)
    row = lax.broadcasted_iota(jnp.int32, (RING * CAP, lanes), 0)
    lane = lax.broadcasted_iota(jnp.int32, (RING * CAP, lanes), 1)
    block = (rank == (row % CAP)[None]) & (row // CAP == lane // tok)[None]
    pick = block.astype(jnp.bfloat16).reshape(-1, lanes)
    weight = weight.reshape(NX, 1, lanes)
    high = lax.reduce_precision(weight, 8, 7)
    parts = []
    for part in (high, weight - high):
        spread = jnp.where(block, part, 0.0).astype(jnp.bfloat16)
        parts.append(spread.reshape(-1, lanes))
    return pick, parts


def picked(plan, normed):
    width = normed.shape[-1]
    rows = jnp.dot(plan[0], normed.reshape(-1, width), preferred_element_type=jnp.float32)
    return rows.astype(jnp.bfloat16).reshape(RING, -1, width)


def expert_rows(rows, gate_up, down):
    blocks, count, width = rows.shape
    rows = rows.reshape(-1, width)
    dims = (((1,), (1,)), ((), ()))
    hidden = lax.dot_general(rows, gate_up, dims, preferred_element_type=jnp.float32)
    units = down.shape[0]
    activated = (jax.nn.silu(hidden[:, :units]) * hidden[:, units:]).astype(jnp.bfloat16)
    out = jnp.dot(activated, down, preferred_element_type=jnp.float32)
    return out.astype(jnp.bfloat16).reshape(blocks, count, width)


def combined(plan, back):
    width = back.shape[-1]
    back = back.reshape(-1, width)
    dims = (((0,), (0,)), ((), ()))
    moe = sum(
        lax.dot_general(part, back, dims, preferred_element_type=jnp.float32) for part in plan[1]
    )
    return moe.astype(jnp.bfloat16).reshape(RING, -1, width)


def finished(hidden, own, partial):
    moe = jnp.sum(partial.astype(jnp.float32), axis=0) + own[0].astype(jnp.float32)
    return (hidden.astype(jnp.float32) + moe).astype(jnp.bfloat16)


X_THERE = (("x", "swap"),)
X_BACK = (("x", "back"),)
Z_BACK = (("z", "reduce"),)
START = (("z", "gather"), ("z", "gather"))
GATHER = (("x", "back"), ("z", "gather"))
RETURN = (("x", "swap"), ("z", "reduce"))


def body(
    fwd_state,
    rev_state,
    norm_gain,
    gate_weight,
    up_weight,
    down_weight,
    fwd_routes,
    rev_routes,
    fwd_combine,
    rev_combine,
):
    index = lax.axis_index("expert")
    x_index = index // NZ
    half = (index % NZ) // (NZ // 2)
    gain_row = norm_gain[0]
    tok = fwd_state.shape[1]
    tables = [a[:, 0].astype(jnp.float32) for a in (fwd_routes, rev_routes, fwd_combine, rev_combine)]
    table = jnp.stack(tables).transpose(0, 1, 3, 2).reshape(-1, tok)
    table = jnp.pad(table, ((0, 0), (0, 128 - tok)))
    fwd, rev = fwd_state[0], rev_state[0]
    fwd_rows, table = exchange(1, START, normed_rows(fwd, gain_row), table)
    mine = (gate_weight[0].T, up_weight[0].T, down_weight[0])
    mine, rev, fwd_rows, table = lax.optimization_barrier((mine, rev, fwd_rows, table))
    gate, up, down = [(one, from_partner(one)) for one in mine]
    weights = lax.optimization_barrier((jnp.concatenate(gate + up), jnp.concatenate(down)))
    table = table[:, :, :tok].reshape(RING, 4, TICKS, 2, tok)

    def plan(stream, tick):
        ids = table[:, stream, tick].astype(jnp.int32)
        return routing(ids, table[:, 2 + stream, tick], x_index, half)

    fwd_plan, rev_plan = plan(0, 0), plan(1, 0)
    (fwd_rows,) = exchange(2, X_THERE, picked(fwd_plan, fwd_rows))
    for tick in range(TICKS):
        fwd_rows, rev_rows = exchange(
            3, GATHER, expert_rows(fwd_rows, *weights), normed_rows(rev, gain_row)
        )
        own = combined(fwd_plan, fwd_rows)
        rows = picked(rev_plan, rev_rows)
        if tick + 1 < TICKS:
            rev_rows, fwd_rows, carry = exchange(7, RETURN, rows, own, fwd, shift=1)
            fwd = finished(carry[0], carry[1:], fwd_rows)
            fwd_plan = plan(0, tick + 1)
            rev_rows, fwd_rows = exchange(
                3, GATHER, expert_rows(rev_rows, *weights), normed_rows(fwd, gain_row)
            )
            own = combined(rev_plan, rev_rows)
            rows = picked(fwd_plan, fwd_rows)
            fwd_rows, rev_rows, carry = exchange(8, RETURN, rows, own, rev, shift=-1)
            rev = finished(carry[0], carry[1:], rev_rows)
            rev_plan = plan(1, tick + 1)
        else:
            rev_rows, fwd_rows = exchange(4, RETURN, rows, own)
            fwd = finished(fwd, own, fwd_rows)
            (rev_rows,) = exchange(6, X_BACK, expert_rows(rev_rows, *weights))
            own = combined(rev_plan, rev_rows)
            (rev_rows,) = exchange(5, Z_BACK, own)
            rev = finished(rev, own, rev_rows)
    return (fwd[None], rev[None])


def solution(mesh):
    placed = (
        P("pipe", "expert", None),
        P("pipe", "expert", None),
        P("pipe", None),
        P("pipe", None, "expert"),
        P("pipe", None, "expert"),
        P("pipe", "expert", None),
        P(None, "pipe", "expert", None),
        P(None, "pipe", "expert", None),
        P(None, "pipe", "expert", None),
        P(None, "pipe", "expert", None),
    )
    return jax.shard_map(
        body,
        mesh=mesh,
        in_specs=placed,
        out_specs=(P("pipe", "expert", None), P("pipe", "expert", None)),
        check_vma=False,
    )
```
